256 devices in a mesh: clu: 128 (over z, y, x), rep: 2 (over core).
Axes of the slice: x: 4, y: 4, z: 8, core: 2. Of those that a mesh axis runs over, the one named last changes fastest.
Arguments:
- current: float32 [256, 2, 2, 2048], P('clu', None, 'rep'), may hold values from -6 to 6
- factors: float32 [512, 2, 2, 128, 2048], P(('clu', 'rep')), may hold values from -0.0625 to 0.0625
- ranks: int32 [512], P(('clu', 'rep')), may hold values from 8 to 40
- pair_clusters: int32 [512, 2], replicated, may hold values from 0 to 255, as said below
Outputs:
- field: float32 [256, 2, 2, 2048], P('clu', None, 'rep')
The draws below stay inside these ranges and needn't reach their ends.
Inputs may be any that keep to these rules, and one draw needn't show every extreme that they name: `pair_clusters`: the 4 cluster ids of the pairs of one device (pairs in blocks of 2 in order) are all different.
All inputs are finite; a program needn't handle non-finite values.
Results may differ from the reference program's by a relative error of at most 0.0003.
Values sent between devices are 32-bit elements; how exact they have to be, the bound alone decides.
A program may use at most 128 MiB of HBM per device.

```python
import jax
import jax.numpy as jnp
from jax import lax

CS = 2048
RPAD = 128
NRHS = 2
PAIR_DEV = 2
NCLU = 256
PAIRS = 512


def draw_pair_clusters(key, part):
    blocks = PAIRS // PAIR_DEV
    end_count = 2 * PAIR_DEV

    def draw_block(block_key):
        order = jax.random.permutation(block_key, NCLU)
        return order[:end_count].astype(jnp.int32)
    block_keys = jax.vmap(lambda block: jax.random.fold_in(key, block))(jnp.arange(blocks, dtype=jnp.int32))
    return jax.vmap(draw_block)(block_keys).reshape(PAIRS, 2).astype(jnp.int32)


def place_ends(drawn, rng, least, largest):
    longest = drawn.shape.index(max(drawn.shape))
    spots = []
    for shift in (0, 1):
        where = [jax.random.randint(jax.random.fold_in(rng, axis), (), 0, length) for axis, length in enumerate(drawn.shape)]
        where[longest] = (where[longest] + shift) % drawn.shape[longest]
        spots.append(tuple(where))
    return drawn.at[spots[0]].set(least).at[spots[1]].set(largest)


def shard_levels(stream_key, extent, cuts, smallest, top_value):
    level, own = 1.0, jax.random.fold_in(stream_key, 6)
    for dim, shards_of in cuts:
        draws = jnp.exp(jax.random.uniform(jax.random.fold_in(own, dim), (shards_of,), jnp.float32, smallest / len(cuts), top_value / len(cuts)))
        level = level * jnp.repeat(draws, extent[dim] // shards_of).reshape([-1 if axis == dim else 1 for axis in range(len(extent))])
    return level


def centred(key, extent, scale, reach, pieces=(), held_as=jnp.bfloat16):
    drawn = scale * jax.random.normal(key, extent, jnp.float32)
    if pieces:
        drawn = drawn * shard_levels(key, extent, pieces, -0.22, 0.18)
    return jnp.clip(drawn, -reach, reach).astype(held_as)


def setup_inputs(seed: int = 0) -> dict:
    key_of = jax.random.split(jax.random.key(seed), 5)
    return {
        "current": centred(key_of[0], (NCLU, 2, NRHS, CS), 1.0, 6.0, ((0, 128), (2, 2)), jnp.float32),
        "factors": centred(key_of[1], (PAIRS, 2, 2, RPAD, CS), (4 * CS) ** -0.5, 0.0625, ((0, 256),), jnp.float32),
        "ranks": place_ends(jax.random.randint(key_of[2], (PAIRS,), RPAD // 16, RPAD * 5 // 16 + 1), jax.random.fold_in(key_of[2], 1), RPAD // 16, (RPAD * 5 // 16 + 1) - 1).astype(jnp.int32),
        "pair_clusters": draw_pair_clusters(jax.random.fold_in(key_of[4], 71), 0),
    }


def project_rows(factor, vector, rank_mask):
    high = lax.Precision.HIGHEST
    real_part = jnp.einsum('prc,pkc->prk', factor[:, 0], vector[:, 0], precision=high) - jnp.einsum('prc,pkc->prk', factor[:, 1], vector[:, 1], precision=high)
    imag_part = jnp.einsum('prc,pkc->prk', factor[:, 0], vector[:, 1], precision=high) + jnp.einsum('prc,pkc->prk', factor[:, 1], vector[:, 0], precision=high)
    return jnp.stack((real_part, imag_part), axis=1) * rank_mask[:, None, :, None]


def expand_rows(factor, projected):
    high = lax.Precision.HIGHEST
    real_part = jnp.einsum('prc,prk->pkc', factor[:, 0], projected[:, 0], precision=high) - jnp.einsum('prc,prk->pkc', factor[:, 1], projected[:, 1], precision=high)
    imag_part = jnp.einsum('prc,prk->pkc', factor[:, 0], projected[:, 1], precision=high) + jnp.einsum('prc,prk->pkc', factor[:, 1], projected[:, 0], precision=high)
    return jnp.stack((real_part, imag_part), axis=1)


def pair_terms(factor_block, rank_list, row_current, col_current):
    left_factor = factor_block[:, 0]
    right_factor = factor_block[:, 1]
    rank_mask = (jnp.arange(factor_block.shape[3], dtype=jnp.int32)[None, :] < rank_list[:, None]).astype(factor_block.dtype)
    row_terms = expand_rows(left_factor, project_rows(right_factor, col_current, rank_mask))
    col_terms = expand_rows(right_factor, project_rows(left_factor, row_current, rank_mask))
    return row_terms, col_terms


def reference(current, factors, ranks, pair_clusters):
    blocks = PAIRS // PAIR_DEV
    result_field = jnp.zeros_like(current)

    def accumulate(result_field, block):
        offset_rows = (block * PAIR_DEV).astype(jnp.int32)
        factor_block = lax.dynamic_slice_in_dim(factors, offset_rows, PAIR_DEV, 0)
        rank_list = lax.dynamic_slice_in_dim(ranks, offset_rows, PAIR_DEV, 0)
        cluster_ids = lax.dynamic_slice_in_dim(pair_clusters, offset_rows, PAIR_DEV, 0)
        row_terms, col_terms = pair_terms(factor_block, rank_list, current[cluster_ids[:, 0]], current[cluster_ids[:, 1]])
        result_field = result_field.at[cluster_ids[:, 0]].add(row_terms)
        result_field = result_field.at[cluster_ids[:, 1]].add(col_terms)
        return result_field, None

    result_field, _ = lax.scan(accumulate, result_field, jnp.arange(blocks, dtype=jnp.int32))
    return result_field
```

```python
import functools

import jax
import jax.numpy as jnp
from jax import lax
from jax.experimental import pallas as pl
from jax.experimental.pallas import tpu as pltpu
from jax.sharding import PartitionSpec as P

MESH = pl.DeviceIdType.MESH
LANES = 128
RANK_ROWS = 64
F32, BF16 = jnp.float32, jnp.bfloat16


def near_last(count):
    return sorted(range(1, count), key=lambda d: (-min(d, count - d), d))


def kernel(
    dims, ids_ref, ranks_ref, cur_ref, fac_ref, out_ref,
    pool, packed, refs, vecs, split, vec8, contrib, items, sums, terms, partial, parts, fac_buf,
    z_send, z_recv, d_send, d_recv, s_send, s_recv, c_send, c_recv, r_send, r_recv, y_send, y_recv, fac_sem,
):
    lz, ly, lx = dims
    side = (ly, lx)
    cross = (lx, ly)
    rows = cur_ref.shape[2]
    clu, rep = lax.axis_index("clu"), lax.axis_index("rep")
    other = 1 - rep
    mx, my, mz = lax.rem(clu, lx), lax.rem(lax.div(clu, lx), ly), lax.div(clu, lx * ly)

    def chip(dx=0, dy=0, dz=0):
        x, y, z = lax.rem(mx + dx, lx), lax.rem(my + dy, ly), lax.rem(mz + dz, lz)
        return (z * ly + y) * lx + x

    def along_side(half, d):
        return chip(dy=d % ly) if half == 0 else chip(dx=d % lx)

    def along_cross(half, d):
        return chip(dx=d % lx) if half == 0 else chip(dy=d % ly)

    def ref_id(at, s):
        return ids_ref[s % 2, at * 4 + s // 2]

    def place(cid):
        owner = lax.div(cid, 2)
        x, y, z = lax.rem(owner, lx), lax.rem(lax.div(owner, lx), ly), lax.div(owner, lx * ly)
        return x, y, z, lax.rem(cid, 2)

    def remote(src, dst, ssem, rsem, to, core):
        return pltpu.make_async_remote_copy(
            src_ref=src, dst_ref=dst, send_sem=ssem, recv_sem=rsem, device_id=(to, core), device_id_type=MESH
        )

    fac_copies = []
    for p in range(2):
        for e in range(2):
            copy = pltpu.make_async_copy(
                fac_ref.at[p, e, :, pl.ds(0, RANK_ROWS), :], fac_buf.at[p * 2 + e], fac_sem.at[p * 2 + e]
            )
            copy.start()
            fac_copies.append(copy)

    barrier = pltpu.get_barrier_semaphore()
    peers = [(clu, other)]
    peers += [(chip(dz=d), rep) for d in range(1, lz)]
    for half in range(2):
        for d in range(1, cross[half]):
            peers += [(along_cross(half, d), rep), (along_cross(half, d), other)]
    for peer in peers:
        pl.semaphore_signal(barrier, inc=1, device_id=peer, device_id_type=MESH)
    for half in range(2):
        for cl in range(2):
            pool[half, cl] = cur_ref[cl, half]
    pl.semaphore_wait(barrier, len(peers))

    z_copies = {}
    for d in near_last(lz):
        z_copies[d] = remote(
            pool.at[:, pl.ds(0, 2)], pool.at[:, pl.ds(2 * d, 2)], z_send.at[d], z_recv.at[d], chip(dz=d), rep
        )
        z_copies[d].start()

    def forward(dz):
        for half in range(2):
            for d in near_last(side[half]):
                remote(
                    pool.at[half, pl.ds(2 * dz, 2)], pool.at[half, pl.ds((d * lz + dz) * 2, 2)],
                    d_send.at[half, d], d_recv.at[half, d], along_side(half, d), rep,
                ).start()

    def split_factor(f):
        fac_copies[f].wait()
        for part in range(2):
            value = fac_buf[f, part]
            high = value.astype(BF16)
            split[f, pl.ds(part * RANK_ROWS, RANK_ROWS), :] = high
            split[f, pl.ds((2 + part) * RANK_ROWS, RANK_ROWS), :] = (value - high.astype(F32)).astype(BF16)

    forward(0)
    split_factor(0)
    split_factor(1)
    arrival = near_last(lz)[::-1]
    for n, dz in enumerate(arrival):
        z_copies[dz].wait_recv()
        forward(dz)
        if n == len(arrival) // 2:
            split_factor(2)
    split_factor(3)
    for half in range(2):
        for d in range(1, side[half]):
            whole = pool.at[half, pl.ds(d * lz * 2, lz * 2)]
            pltpu.make_async_copy(whole, whole, d_recv.at[half, d]).wait()

    s_copies = []
    for half in range(2):
        for d in near_last(cross[half]) + [0]:
            to = along_cross(half, d)
            for s in range(8):
                x, y, z, cl = place(ref_id(to, s))
                shift = lax.rem((my - y if half == 0 else mx - x) + side[half], side[half])
                slot = (shift * lz + lax.rem(mz - z + lz, lz)) * 2 + cl
                packed[half, d, s // 4, s % 4] = pool[half, slot]
            for q, core in ((0, rep), (1, other)):
                if d == 0 and q == 0:
                    refs[half, 0, rep] = packed[half, 0, rep]
                    continue
                copy = remote(
                    packed.at[half, d, core], refs.at[half, d, rep],
                    s_send.at[half, d, q], s_recv.at[half, d, q], to, core,
                )
                copy.start()
                s_copies.append(copy)

    lane = lax.broadcasted_iota(jnp.int32, (8, LANES), 1)
    placers = []
    for half in range(2):
        target = jnp.full((8, LANES), -1, jnp.int32)
        for d in range(cross[half]):
            source = along_cross(half, cross[half] - d)
            for s in range(8):
                x, y, z, cl = place(ref_id(source, s))
                mine = (x == mx) if half == 0 else (y == my)
                shift = lax.rem((y - my if half == 0 else x - mx) + side[half], side[half])
                slot = (shift * lz + lax.rem(z - mz + lz, lz)) * 2 + cl
                slot = jnp.where(mine, slot, -1)
                at = d * 8 + s
                target = jnp.where((lane == at) | (lane == at + 8 * cross[half]), slot, target)
        slots = side[half] * lz * 2
        wide = jnp.concatenate([target] * (slots // 8), axis=0)[:, : 16 * cross[half]]
        placers.append(
            jnp.where(lax.broadcasted_iota(jnp.int32, wide.shape, 0) == wide, 1.0, 0.0).astype(BF16)
        )

    for copy in s_copies:
        copy.wait_recv()

    row = lax.broadcasted_iota(jnp.int32, (8, LANES), 0)
    col = lax.broadcasted_iota(jnp.int32, (8, LANES), 1)
    first = row < 4
    sign = jnp.where(lax.rem(row, 4) < 2, -1.0, 1.0).astype(F32)
    for s in range(4):
        x, y, z, cl = place(ids_ref[s % 2, clu * 4 + rep * 2 + s // 2])
        dx, dy = lax.rem(mx - x + lx, lx), lax.rem(my - y + ly, ly)
        for k in range(2):
            for half, d in ((0, dx), (1, dy)):
                value = refs[half, d, k, s]
                vecs[s, pl.ds((half * 2 + k) * rows, rows), :] = value
                vecs[s, pl.ds((4 + half * 2 + k) * rows, rows), :] = value
    for s in range(4):
        p, e = s // 2, s % 2
        for j in range(rows):
            value = vecs[s, pl.ds(j, 8, stride=rows), :]
            high = value.astype(BF16).astype(F32)
            vec8[s, :, pl.ds(j * LANES, LANES)] = jnp.where(first, high, value - high).astype(BF16)
        got = lax.dot_general(
            vec8[s], split[p * 2 + e], (((1,), (1,)), ((), ())), preferred_element_type=F32
        )
        both = got[:, :LANES] + got[:, LANES:]
        both = both + pltpu.roll(both, 4, 0)
        t = both + sign * pltpu.roll(pltpu.roll(both, RANK_ROWS, 1), 2, 0)
        t = jnp.where(col < jnp.minimum(ranks_ref[p], RANK_ROWS), t, 0.0)
        t = t + pltpu.roll(sign * pltpu.roll(t, 2, 0), RANK_ROWS, 1)
        high = t.astype(BF16).astype(F32)
        t = jnp.where(first, high, t - high).astype(BF16)
        t = jnp.concatenate([t, t], axis=1)
        target = p * 2 + 1 - e
        for j in range(rows // 2):
            out = jnp.dot(
                t, split[p * 2 + 1 - e, :, pl.ds(j * 2 * LANES, 2 * LANES)], preferred_element_type=F32
            )
            for i in range(2):
                block = out[:, i * LANES : (i + 1) * LANES]
                block = block + pltpu.roll(block, 4, 0)
                contrib[pl.ds(target * rows + 2 * j + i, 4, stride=4 * rows), :] = block[:4]

    span = 4 * rows
    c_copies = []
    for half in range(2):
        for d in near_last(cross[half]) + [0]:
            to = along_cross(half, d)
            for q, core in ((0, rep), (1, other)):
                start = pl.multiple_of((half * 2 + core) * span, span)
                if d == 0 and q == 0:
                    items[half, pl.ds(pl.multiple_of(rep * span, span), span), :] = contrib[pl.ds(start, span), :]
                    continue
                copy = remote(
                    contrib.at[pl.ds(start, span), :],
                    items.at[half, pl.ds(pl.multiple_of(d * 2 * span + rep * span, span), span), :],
                    c_send.at[half, d, q], c_recv.at[half, d, q], to, core,
                )
                copy.start()
                c_copies.append((half, copy))

    order = near_last(lz) + [0]
    block = 2 * rows
    for half in range(2):
        for h, copy in c_copies:
            if h == half:
                copy.wait_recv()
        slots = side[half] * lz * 2
        for j in range(0, rows, 2):
            value = jnp.concatenate(
                [
                    jnp.concatenate(
                        [items[half, pl.ds(d * 8 * rows + j + i, 8, stride=rows), :] for d in range(cross[half])],
                        axis=0,
                    )
                    for i in range(2)
                ],
                axis=1,
            )
            high = value.astype(BF16)
            low = (value - high.astype(F32)).astype(BF16)
            total = jnp.dot(
                placers[half], jnp.concatenate([high, low], axis=0), preferred_element_type=F32
            )
            for g in range(slots // 8):
                for i in range(2):
                    sums[half, pl.ds(g * 8 * rows + j + i, 8, stride=rows), :] = total[
                        g * 8 : g * 8 + 8, i * LANES : (i + 1) * LANES
                    ]
        for dz in order:
            for d in near_last(side[half]):
                remote(
                    sums.at[half, pl.ds((d * lz + dz) * block, block), :], terms.at[dz, half, d - 1],
                    r_send.at[half, d], r_recv.at[dz], along_side(half, d), rep,
                ).start()

    y_copies = []
    for dz in order:
        pltpu.make_async_copy(terms.at[dz], terms.at[dz], r_recv.at[dz]).wait()
        for half in range(2):
            value = sums[half, pl.ds(dz * block, block), :]
            for d in range(1, side[half]):
                value = value + terms[dz, half, d - 1]
            (parts if dz == 0 else partial)[dz, half] = value
        if dz:
            copy = remote(partial.at[dz], parts.at[dz], y_send.at[dz], y_recv.at[dz], chip(dz=dz), rep)
            copy.start()
            y_copies.append(copy)
    for copy in y_copies:
        copy.wait_recv()
    for half in range(2):
        for cl in range(2):
            value = parts[0, half, pl.ds(cl * rows, rows), :]
            for dz in range(1, lz):
                value = value + parts[dz, half, pl.ds(cl * rows, rows), :]
            out_ref[cl, half] = value

    for copy in list(z_copies.values()) + s_copies + [c for _, c in c_copies] + y_copies:
        copy.wait_send()
    for half in range(2):
        for d in range(1, side[half]):
            whole = pool.at[half, pl.ds(0, lz * 2)]
            pltpu.make_async_copy(whole, whole, d_send.at[half, d]).wait()
            whole = sums.at[half, pl.ds(d * lz * block, lz * block), :]
            pltpu.make_async_copy(whole, whole, r_send.at[half, d]).wait()


def local(dims, current, factors, ranks, pair_clusters):
    lz, ly, lx = dims
    unknowns = current.shape[3]
    rows = unknowns // LANES
    line = max(lx, ly)
    plane = 2 * lz * line
    dma = pltpu.SemaphoreType.DMA
    smem, vmem = pl.BlockSpec(memory_space=pltpu.SMEM), pl.BlockSpec(memory_space=pltpu.VMEM)
    field = pl.pallas_call(
        functools.partial(kernel, dims),
        out_shape=jax.ShapeDtypeStruct((2, 2, rows, LANES), F32),
        in_specs=[smem, smem, vmem, pl.BlockSpec(memory_space=pl.ANY)],
        out_specs=vmem,
        scratch_shapes=[
            pltpu.VMEM((2, plane, rows, LANES), F32),
            pltpu.VMEM((2, line, 2, 4, rows, LANES), F32),
            pltpu.VMEM((2, line, 2, 4, rows, LANES), F32),
            pltpu.VMEM((4, 8 * rows, LANES), F32),
            pltpu.VMEM((4, 4 * RANK_ROWS, unknowns), BF16),
            pltpu.VMEM((4, 8, unknowns), BF16),
            pltpu.VMEM((16 * rows, LANES), F32),
            pltpu.VMEM((2, line * 8 * rows, LANES), F32),
            pltpu.VMEM((2, plane * rows, LANES), F32),
            pltpu.VMEM((lz, 2, line - 1, 2 * rows, LANES), F32),
            pltpu.VMEM((lz, 2, 2 * rows, LANES), F32),
            pltpu.VMEM((lz, 2, 2 * rows, LANES), F32),
            pltpu.VMEM((4, 2, RANK_ROWS, unknowns), F32),
            dma((lz,)), dma((lz,)),
            dma((2, line)), dma((2, line)),
            dma((2, line, 2)), dma((2, line, 2)),
            dma((2, line, 2)), dma((2, line, 2)),
            dma((2, line)), dma((lz,)),
            dma((lz,)), dma((lz,)),
            dma((4,)),
        ],
        compiler_params=pltpu.CompilerParams(
            collective_id=0, has_side_effects=True, vmem_limit_bytes=48 * 1024 * 1024
        ),
    )(pair_clusters.T, ranks, current.reshape(2, 2, rows, LANES), factors)
    return field.reshape(current.shape)


def solution(mesh, dims=(8, 4, 4)):
    placed = (
        P("clu", None, "rep", None),
        P(("clu", "rep"), None, None, None, None),
        P(("clu", "rep")),
        P(),
    )
    return jax.shard_map(
        functools.partial(local, dims), mesh=mesh, in_specs=placed,
        out_specs=P("clu", None, "rep", None), check_vma=False,
    )
```

```python
import functools

import jax
import jax.numpy as jnp
from jax import lax
from jax.experimental import pallas as pl
from jax.experimental.pallas import tpu as pltpu
from jax.sharding import PartitionSpec as P

MESH = pl.DeviceIdType.MESH
LANES = 128
RANK_ROWS = 64
F32, BF16 = jnp.float32, jnp.bfloat16


def near_last(count):
    return sorted(range(1, count), key=lambda d: (-min(d, count - d), d))


def kernel(
    dims, ids_hbm, ranks_hbm, cur_ref, fac_ref, out_ref,
    ids_ref, ranks_ref, slots_ref,
    pool, packed, refs0, refs1, vecs, split, vec8, contrib0, contrib1, items, sums, terms, partial, parts, fac_buf,
    z_send, z_recv, d_send, d_recv, s_send, s_recv, c_send, c_recv, r_send, r_recv, y_send, y_recv, fac_sem, in_sem,
):
    lz, ly, lx = dims
    side = (ly, lx)
    cross = (lx, ly)
    rows = cur_ref.shape[2]
    clu, rep = lax.axis_index("clu"), lax.axis_index("rep")
    other = 1 - rep
    mx, my, mz = lax.rem(clu, lx), lax.rem(lax.div(clu, lx), ly), lax.div(clu, lx * ly)

    def chip(dx=0, dy=0, dz=0):
        x, y, z = lax.rem(mx + dx, lx), lax.rem(my + dy, ly), lax.rem(mz + dz, lz)
        return (z * ly + y) * lx + x

    def along_side(half, d):
        return chip(dy=d % ly) if half == 0 else chip(dx=d % lx)

    def along_cross(half, d):
        return chip(dx=d % lx) if half == 0 else chip(dy=d % ly)

    def ref_id(at, s):
        return ids_ref[s % 2, at * 4 + s // 2]

    def place(cid):
        bx, by = lx.bit_length() - 1, ly.bit_length() - 1
        return (cid >> 1) & (lx - 1), (cid >> (1 + bx)) & (ly - 1), cid >> (1 + bx + by), cid & 1

    def remote(src, dst, ssem, rsem, to, core):
        return pltpu.make_async_remote_copy(
            src_ref=src, dst_ref=dst, send_sem=ssem, recv_sem=rsem, device_id=(to, core), device_id_type=MESH
        )

    barrier = pltpu.get_barrier_semaphore()
    peers = [(clu, other)]
    peers += [(chip(dz=d), rep) for d in range(1, lz)]
    for half in range(2):
        for d in range(1, cross[half]):
            peers += [(along_cross(half, d), rep), (along_cross(half, d), other)]
    for peer in peers:
        pl.semaphore_signal(barrier, inc=1, device_id=peer, device_id_type=MESH)
    own_copies = []
    for half in range(2):
        copy = pltpu.make_async_copy(cur_ref.at[:, half], pool.at[half, pl.ds(0, 2)], in_sem.at[half])
        copy.start()
        own_copies.append(copy)
    table_copies = [
        pltpu.make_async_copy(ids_hbm, ids_ref, in_sem.at[2]), pltpu.make_async_copy(ranks_hbm, ranks_ref, in_sem.at[3])
    ]
    for copy in table_copies:
        copy.start()
    fac_copies = []
    for p in range(2):
        for e in range(2):
            copy = pltpu.make_async_copy(
                fac_ref.at[p, e, :, pl.ds(0, RANK_ROWS), :], fac_buf.at[p * 2 + e], fac_sem.at[p * 2 + e]
            )
            copy.start()
            fac_copies.append(copy)
    for copy in own_copies:
        copy.wait()
    pl.semaphore_wait(barrier, len(peers))

    arrival = near_last(lz)[::-1]
    z_copies = {}
    for d in arrival:
        z_copies[d] = remote(
            pool.at[:, pl.ds(0, 2)], pool.at[:, pl.ds(2 * d, 2)], z_send.at[d], z_recv.at[d], chip(dz=d), rep
        )
        z_copies[d].start()

    def forward(dz):
        for d in near_last(max(side)):
            for half in range(2):
                if d >= side[half]:
                    continue
                remote(
                    pool.at[half, pl.ds(2 * dz, 2)], pool.at[half, pl.ds((d * lz + dz) * 2, 2)],
                    d_send.at[half, d], d_recv.at[half, d], along_side(half, d), rep,
                ).start()

    def split_factor(f):
        fac_copies[f].wait()
        for part in range(2):
            value = fac_buf[f, part]
            high = value.astype(BF16)
            split[f, pl.ds(part * RANK_ROWS, RANK_ROWS), :] = high
            split[f, pl.ds((2 + part) * RANK_ROWS, RANK_ROWS), :] = (value - high.astype(F32)).astype(BF16)

    def find_slots(half):
        for d in range(cross[half]):
            to = along_cross(half, d)
            for s in range(8):
                x, y, z, cl = place(ref_id(to, s))
                shift = (my - y if half == 0 else mx - x) & (side[half] - 1)
                slots_ref[(half * cross[half] + d) * 8 + s] = (shift * lz + ((mz - z) & (lz - 1))) * 2 + cl

    lane = lax.broadcasted_iota(jnp.int32, (8, LANES), 1)

    def make_placer(half):
        target = jnp.full((8, LANES), -1, jnp.int32)
        for d in range(cross[half]):
            source = along_cross(half, cross[half] - d)
            for s in range(8):
                x, y, z, cl = place(ref_id(source, s))
                mine = (x == mx) if half == 0 else (y == my)
                shift = (y - my if half == 0 else x - mx) & (side[half] - 1)
                slot = (shift * lz + ((z - mz) & (lz - 1))) * 2 + cl
                slot = jnp.where(mine, slot, -1)
                at = d * 8 + s
                target = jnp.where((lane == at) | (lane == at + 8 * cross[half]), slot, target)
        slots = side[half] * lz * 2
        wide = jnp.concatenate([target] * (slots // 8), axis=0)[:, : 16 * cross[half]]
        return jnp.where(lax.broadcasted_iota(jnp.int32, wide.shape, 0) == wide, 1.0, 0.0).astype(BF16)

    forward(0)
    for copy in table_copies:
        copy.wait()
    find_slots(0)
    find_slots(1)
    for n, dz in enumerate(arrival):
        z_copies[dz].wait_recv()
        forward(dz)
        if n == 1 % len(arrival):
            split_factor(0)
            split_factor(1)
        if n == 3 % len(arrival):
            split_factor(2)
            split_factor(3)
    placers = [make_placer(0), make_placer(1)]
    for half in range(2):
        for d in range(1, side[half]):
            whole = pool.at[half, pl.ds(d * lz * 2, lz * 2)]
            pltpu.make_async_copy(whole, whole, d_recv.at[half, d]).wait()

    refs = (refs0, refs1)
    s_copies = ([], [])
    for p in range(2):
        for d in near_last(max(cross)) + [0]:
            for half in range(2):
                if d >= cross[half]:
                    continue
                for core in range(2):
                    for s in (2 * p, 2 * p + 1):
                        packed[half, d, core, s] = pool[
                            half, slots_ref[(half * cross[half] + d) * 8 + core * 4 + s]
                        ]
                for q, core in ((0, rep), (1, other)):
                    if d == 0 and q == 0:
                        for s in (2 * p, 2 * p + 1):
                            refs[p][half, 0, rep, s % 2] = packed[half, 0, rep, s]
                        continue
                    copy = remote(
                        packed.at[half, d, core, pl.ds(2 * p, 2)], refs[p].at[half, d, rep],
                        s_send.at[p, half, d, q], s_recv.at[p, half, d, q], along_cross(half, d), core,
                    )
                    copy.start()
                    s_copies[p].append(copy)

    row = lax.broadcasted_iota(jnp.int32, (8, LANES), 0)
    col = lax.broadcasted_iota(jnp.int32, (8, LANES), 1)
    first = row < 4
    sign = jnp.where(lax.rem(row, 4) < 2, -1.0, 1.0).astype(F32)
    span = 4 * rows
    contrib = (contrib0, contrib1)
    c_copies = []
    for p in range(2):
        for copy in s_copies[p]:
            copy.wait_recv()
        for s in (2 * p, 2 * p + 1):
            x, y, z, cl = place(ids_ref[s % 2, clu * 4 + rep * 2 + p])
            dx, dy = (mx - x) & (lx - 1), (my - y) & (ly - 1)
            for k in range(2):
                for half, d in ((0, dx), (1, dy)):
                    value = refs[p][half, d, k, s % 2]
                    vecs[s, pl.ds((half * 2 + k) * rows, rows), :] = value
                    vecs[s, pl.ds((4 + half * 2 + k) * rows, rows), :] = value
        for e in range(2):
            s = 2 * p + e
            for j in range(rows):
                value = vecs[s, pl.ds(j, 8, stride=rows), :]
                high = value.astype(BF16).astype(F32)
                vec8[s, :, pl.ds(j * LANES, LANES)] = jnp.where(first, high, value - high).astype(BF16)
            got = lax.dot_general(
                vec8[s], split[p * 2 + e], (((1,), (1,)), ((), ())), preferred_element_type=F32
            )
            both = got[:, :LANES] + got[:, LANES:]
            both = both + pltpu.roll(both, 4, 0)
            t = both + sign * pltpu.roll(pltpu.roll(both, RANK_ROWS, 1), 2, 0)
            t = jnp.where(col < jnp.minimum(ranks_ref[p], RANK_ROWS), t, 0.0)
            t = t + pltpu.roll(sign * pltpu.roll(t, 2, 0), RANK_ROWS, 1)
            high = t.astype(BF16).astype(F32)
            t = jnp.where(first, high, t - high).astype(BF16)
            t = jnp.concatenate([t, t], axis=1)
            target = 1 - e
            for j in range(rows // 2):
                out = jnp.dot(
                    t, split[p * 2 + 1 - e, :, pl.ds(j * 2 * LANES, 2 * LANES)], preferred_element_type=F32
                )
                for i in range(2):
                    block = out[:, i * LANES : (i + 1) * LANES]
                    block = block + pltpu.roll(block, 4, 0)
                    contrib[p][pl.ds(target * rows + 2 * j + i, 4, stride=2 * rows), :] = block[:4]
        for d in near_last(max(cross)) + [0]:
            for half in range(2):
                if d >= cross[half]:
                    continue
                for q, core in ((0, rep), (1, other)):
                    start = pl.multiple_of((half * 2 + core) * 2 * rows, rows)
                    land = pl.multiple_of((d * 2 + rep) * span + p * 2 * rows, rows)
                    if d == 0 and q == 0:
                        items[half, pl.ds(land, 2 * rows), :] = contrib[p][pl.ds(start, 2 * rows), :]
                        continue
                    copy = remote(
                        contrib[p].at[pl.ds(start, 2 * rows), :], items.at[half, pl.ds(land, 2 * rows), :],
                        c_send.at[p, half, d, q], c_recv.at[p, half, d, q], along_cross(half, d), core,
                    )
                    copy.start()
                    c_copies.append((half, copy))

    order = near_last(lz) + [0]
    block = 2 * rows
    for half in range(2):
        for h, copy in c_copies:
            if h == half:
                copy.wait_recv()
        slots = side[half] * lz * 2
        for j in range(0, rows, 2):
            value = jnp.concatenate(
                [
                    jnp.concatenate(
                        [items[half, pl.ds(d * 8 * rows + j + i, 8, stride=rows), :] for d in range(cross[half])],
                        axis=0,
                    )
                    for i in range(2)
                ],
                axis=1,
            )
            high = value.astype(BF16)
            low = (value - high.astype(F32)).astype(BF16)
            total = jnp.dot(
                placers[half], jnp.concatenate([high, low], axis=0), preferred_element_type=F32
            )
            for g in range(slots // 8):
                for i in range(2):
                    sums[half, pl.ds(g * 8 * rows + j + i, 8, stride=rows), :] = total[
                        g * 8 : g * 8 + 8, i * LANES : (i + 1) * LANES
                    ]
        for dz in order:
            for d in near_last(side[half]):
                remote(
                    sums.at[half, pl.ds((d * lz + dz) * block, block), :], terms.at[dz, half, d - 1],
                    r_send.at[half, d], r_recv.at[dz], along_side(half, d), rep,
                ).start()

    y_copies = []
    for dz in order:
        pltpu.make_async_copy(terms.at[dz], terms.at[dz], r_recv.at[dz]).wait()
        for half in range(2):
            value = sums[half, pl.ds(dz * block, block), :]
            for d in range(1, side[half]):
                value = value + terms[dz, half, d - 1]
            (parts if dz == 0 else partial)[dz, half] = value
        if dz:
            copy = remote(partial.at[dz], parts.at[dz], y_send.at[dz], y_recv.at[dz], chip(dz=dz), rep)
            copy.start()
            y_copies.append(copy)
    for copy in y_copies:
        copy.wait_recv()
    for half in range(2):
        for cl in range(2):
            value = parts[0, half, pl.ds(cl * rows, rows), :]
            for dz in range(1, lz):
                value = value + parts[dz, half, pl.ds(cl * rows, rows), :]
            out_ref[cl, half] = value

    for copy in list(z_copies.values()) + s_copies[0] + s_copies[1] + [c for _, c in c_copies] + y_copies:
        copy.wait_send()
    for half in range(2):
        for d in range(1, side[half]):
            whole = pool.at[half, pl.ds(0, lz * 2)]
            pltpu.make_async_copy(whole, whole, d_send.at[half, d]).wait()
            whole = sums.at[half, pl.ds(d * lz * block, lz * block), :]
            pltpu.make_async_copy(whole, whole, r_send.at[half, d]).wait()


def local(dims, current, factors, ranks, pair_clusters):
    lz, ly, lx = dims
    unknowns = current.shape[3]
    rows = unknowns // LANES
    line = max(lx, ly)
    plane = 2 * lz * line
    dma = pltpu.SemaphoreType.DMA
    field = pl.pallas_call(
        functools.partial(kernel, dims),
        out_shape=jax.ShapeDtypeStruct((2, 2, rows, LANES), F32),
        in_specs=[pl.BlockSpec(memory_space=pltpu.HBM)] * 4,
        out_specs=pl.BlockSpec(memory_space=pltpu.VMEM),
        scratch_shapes=[
            pltpu.SMEM((2, pair_clusters.shape[0]), jnp.int32), pltpu.SMEM(ranks.shape, jnp.int32),
            pltpu.SMEM((16 * line,), jnp.int32),
            pltpu.VMEM((2, plane, rows, LANES), F32),
            pltpu.VMEM((2, line, 2, 4, rows, LANES), F32),
            pltpu.VMEM((2, line, 2, 2, rows, LANES), F32),
            pltpu.VMEM((2, line, 2, 2, rows, LANES), F32),
            pltpu.VMEM((4, 8 * rows, LANES), F32),
            pltpu.VMEM((4, 4 * RANK_ROWS, unknowns), BF16),
            pltpu.VMEM((4, 8, unknowns), BF16),
            pltpu.VMEM((8 * rows, LANES), F32),
            pltpu.VMEM((8 * rows, LANES), F32),
            pltpu.VMEM((2, line * 8 * rows, LANES), F32),
            pltpu.VMEM((2, plane * rows, LANES), F32),
            pltpu.VMEM((lz, 2, line - 1, 2 * rows, LANES), F32),
            pltpu.VMEM((lz, 2, 2 * rows, LANES), F32),
            pltpu.VMEM((lz, 2, 2 * rows, LANES), F32),
            pltpu.VMEM((4, 2, RANK_ROWS, unknowns), F32),
            dma((lz,)), dma((lz,)),
            dma((2, line)), dma((2, line)),
            dma((2, 2, line, 2)), dma((2, 2, line, 2)),
            dma((2, 2, line, 2)), dma((2, 2, line, 2)),
            dma((2, line)), dma((lz,)),
            dma((lz,)), dma((lz,)),
            dma((4,)), dma((4,)),
        ],
        compiler_params=pltpu.CompilerParams(
            collective_id=0, has_side_effects=True, vmem_limit_bytes=48 * 1024 * 1024
        ),
    )(*[
        pltpu.with_memory_space_constraint(operand, pltpu.HBM)
        for operand in (pair_clusters.T, ranks, current.reshape(2, 2, rows, LANES), factors)
    ])
    return field.reshape(current.shape)


def solution(mesh, dims=(8, 4, 4)):
    placed = (
        P("clu", None, "rep", None),
        P(("clu", "rep"), None, None, None, None),
        P(("clu", "rep")),
        P(),
    )
    return jax.shard_map(
        functools.partial(local, dims), mesh=mesh, in_specs=placed,
        out_specs=P("clu", None, "rep", None), check_vma=False,
    )
```

```python
import functools

import jax
import jax.numpy as jnp
from jax import lax
from jax.experimental import pallas as pl
from jax.experimental.pallas import tpu as pltpu
from jax.sharding import PartitionSpec as P

MESH = pl.DeviceIdType.MESH
LANES = 128
RANK_ROWS = 48
F32, BF16 = jnp.float32, jnp.bfloat16


def near_last(count):
    return sorted(range(1, count), key=lambda d: (-min(d, count - d), d))


def kernel(
    dims, ids_hbm, ranks_hbm, cur_ref, fac_ref, out_ref,
    ids_ref, ranks_ref, slots_ref,
    pool, packed, refs, vecs, split, vec8, contrib, items, sums, terms, partial, parts, fac_buf,
    z_send, z_recv, d_send, d_recv, s_send, s_recv, c_send, c_recv, r_send, r_recv, y_send, y_recv, fac_sem, in_sem,
):
    lz, ly, lx = dims
    side = (ly, lx)
    cross = (lx, ly)
    rows = cur_ref.shape[2]
    line = lx
    clu, rep = lax.axis_index("clu"), lax.axis_index("rep")
    other = 1 - rep
    mx, my, mz = lax.rem(clu, lx), lax.rem(lax.div(clu, lx), ly), lax.div(clu, lx * ly)

    def chip(dx=0, dy=0, dz=0):
        x, y, z = lax.rem(mx + dx, lx), lax.rem(my + dy, ly), lax.rem(mz + dz, lz)
        return (z * ly + y) * lx + x

    def along_side(half, d):
        return chip(dy=d % ly) if half == 0 else chip(dx=d % lx)

    def along_cross(half, d):
        return chip(dx=d % lx) if half == 0 else chip(dy=d % ly)

    def ref_id(at, s):
        return ids_ref[s % 2, at * 4 + s // 2]

    def place(cid):
        bx, by = lx.bit_length() - 1, ly.bit_length() - 1
        return (cid >> 1) & (lx - 1), (cid >> (1 + bx)) & (ly - 1), cid >> (1 + bx + by), cid & 1

    def drain(ref, sem):
        pltpu.make_async_copy(ref, ref, sem).wait()

    def remote(src, dst, ssem, rsem, to, core):
        return pltpu.make_async_remote_copy(
            src_ref=src, dst_ref=dst, send_sem=ssem, recv_sem=rsem, device_id=(to, core), device_id_type=MESH
        )

    direct = [d for d in range(1, lz) if min(d, lz - d) <= 2]
    relays = [(3, 2, 1, (0, 1)), (5, 6, 7, (0, 1)), (4, 2, 2, (0,)), (4, 6, 6, (1,))] if lz == 8 else []
    barrier = pltpu.get_barrier_semaphore()
    peers = [(clu, other)]
    peers += [(chip(dz=d), rep) for d in direct]
    for half in range(2):
        for d in range(1, cross[half]):
            peers += [(along_cross(half, d), rep), (along_cross(half, d), other)]
    for peer in peers:
        pl.semaphore_signal(barrier, inc=1, device_id=peer, device_id_type=MESH)
    for half in range(2):
        pltpu.make_async_copy(cur_ref.at[:, half], pool.at[half, pl.ds(0, 2)], in_sem.at[0]).start()
    table_copies = [
        pltpu.make_async_copy(ids_hbm, ids_ref, in_sem.at[1]), pltpu.make_async_copy(ranks_hbm, ranks_ref, in_sem.at[2])
    ]
    for copy in table_copies:
        copy.start()
    fac_copies = []
    for p in range(2):
        for e in range(2):
            copy = pltpu.make_async_copy(
                fac_ref.at[p, e, :, pl.ds(0, RANK_ROWS), :], fac_buf.at[p * 2 + e], fac_sem.at[p * 2 + e]
            )
            copy.start()
            fac_copies.append(copy)
    drain(pool.at[:, pl.ds(0, 2)], in_sem.at[0])
    pl.semaphore_wait(barrier, len(peers))

    arrivals = {}

    def send_along_z(held, lands, step, halves, n):
        part = pl.ds(halves[0], len(halves))
        copy = remote(
            pool.at[part, pl.ds(2 * held, 2)], pool.at[part, pl.ds(2 * lands, 2)],
            z_send, z_recv.at[n], chip(dz=step), rep,
        )
        copy.start()
        arrivals.setdefault(lands, []).append(copy)

    arrival = [d for d in near_last(lz) if d in direct]
    for n, d in enumerate(arrival):
        send_along_z(0, d, d, (0, 1), n)
    arrival += [d for d in (3, 5, 4) if d not in direct and d < lz]

    def forward(dz):
        for d in near_last(max(side)):
            for half in range(2):
                if d >= side[half]:
                    continue
                remote(
                    pool.at[half, pl.ds(2 * dz, 2)], pool.at[half, pl.ds((d * lz + dz) * 2, 2)],
                    d_send, d_recv, along_side(half, d), rep,
                ).start()

    def split_factor(f):
        fac_copies[f].wait()
        for part in range(2):
            value = fac_buf[f, part]
            high = value.astype(BF16)
            split[f, 0, pl.ds(part * RANK_ROWS, RANK_ROWS), :] = high
            split[f, 1, pl.ds(part * RANK_ROWS, RANK_ROWS), :] = (value - high.astype(F32)).astype(BF16)

    def find_slots(half):
        for d in range(cross[half]):
            to = along_cross(half, d)
            for s in range(8):
                x, y, z, cl = place(ref_id(to, s))
                shift = (my - y if half == 0 else mx - x) & (side[half] - 1)
                slots_ref[(half * cross[half] + d) * 8 + s] = (shift * lz + ((mz - z) & (lz - 1))) * 2 + cl

    lane = lax.broadcasted_iota(jnp.int32, (8, LANES), 1)

    def make_placer(half):
        target = jnp.full((8, LANES), -1, jnp.int32)
        for d in range(cross[half]):
            source = along_cross(half, cross[half] - d)
            for s in range(8):
                x, y, z, cl = place(ref_id(source, s))
                mine = (x == mx) if half == 0 else (y == my)
                shift = (y - my if half == 0 else x - mx) & (side[half] - 1)
                slot = (shift * lz + ((z - mz) & (lz - 1))) * 2 + cl
                slot = jnp.where(mine, slot, -1)
                at = d * 8 + s
                target = jnp.where((lane == at) | (lane == at + 8 * cross[half]), slot, target)
        slots = side[half] * lz * 2
        wide = jnp.concatenate([target] * (slots // 8), axis=0)[:, : 16 * cross[half]]
        return jnp.where(lax.broadcasted_iota(jnp.int32, wide.shape, 0) == wide, 1.0, 0.0).astype(BF16)

    forward(0)
    for copy in table_copies:
        copy.wait()
    find_slots(0)
    find_slots(1)
    for n, dz in enumerate(arrival):
        for copy in arrivals[dz]:
            copy.wait_recv()
        for m, (lands, held, step, halves) in enumerate(relays):
            if held == dz:
                send_along_z(held, lands, step, halves, len(direct) + m)
        forward(dz)
        if n == 1 % len(arrival):
            split_factor(0)
            split_factor(1)
        if n == 3 % len(arrival):
            split_factor(2)
            split_factor(3)
    placers = [make_placer(0), make_placer(1)]
    drain(pool.at[:, pl.ds(2 * lz, 2 * lz * (line - 1))], d_recv)

    for s in range(4):
        for d in near_last(max(cross)) + [0]:
            for half in range(2):
                if d >= cross[half]:
                    continue
                for core in range(2):
                    packed[half, d, core, s] = pool[half, slots_ref[(half * cross[half] + d) * 8 + core * 4 + s]]
                for q, core in ((0, rep), (1, other)):
                    if d == 0 and q == 0:
                        refs[s][half, 0, rep] = packed[half, 0, rep, s]
                        continue
                    remote(
                        packed.at[half, d, core, s], refs[s].at[half, d, rep],
                        s_send, s_recv.at[s, min(d, 1)], along_cross(half, d), core,
                    ).start()

    row = lax.broadcasted_iota(jnp.int32, (8, LANES), 0)
    col = lax.broadcasted_iota(jnp.int32, (8, LANES), 1)
    first = row < 4
    sign = jnp.where(lax.rem(row, 4) < 2, -1.0, 1.0).astype(F32)
    for s in range(4):
        p, e = s // 2, s % 2
        x, y, z, cl = place(ids_ref[e, clu * 4 + rep * 2 + p])
        dx, dy = (mx - x) & (lx - 1), (my - y) & (ly - 1)
        drain(refs[s].at[:, pl.ds(1, line - 1)], s_recv.at[s, 1])
        drain(refs[s].at[:, 0, other], s_recv.at[s, 0])
        for k in range(2):
            for half, d in ((0, dx), (1, dy)):
                value = refs[s][half, d, k]
                vecs[s, pl.ds((half * 2 + k) * rows, rows), :] = value
                vecs[s, pl.ds((4 + half * 2 + k) * rows, rows), :] = value
        for j in range(rows):
            value = vecs[s, pl.ds(j, 8, stride=rows), :]
            high = value.astype(BF16).astype(F32)
            vec8[s, :, pl.ds(j * LANES, LANES)] = jnp.where(first, high, value - high).astype(BF16)
        both = sum(
            lax.dot_general(vec8[s], split[s, part], (((1,), (1,)), ((), ())), preferred_element_type=F32)
            for part in range(2)
        )
        both = jnp.concatenate([both, jnp.zeros((8, LANES - 2 * RANK_ROWS), F32)], axis=1)
        both = both + pltpu.roll(both, 4, 0)
        t = both + sign * pltpu.roll(pltpu.roll(both, LANES - RANK_ROWS, 1), 2, 0)
        t = jnp.where(col < jnp.minimum(ranks_ref[p], RANK_ROWS), t, 0.0)
        t = t + pltpu.roll(sign * pltpu.roll(t, 2, 0), RANK_ROWS, 1)
        high = t.astype(BF16).astype(F32)
        t = jnp.where(first, high, t - high).astype(BF16)[:, : 2 * RANK_ROWS]
        target = 2 * p + 1 - e
        for j in range(rows // 2):
            out = sum(
                jnp.dot(t, split[target, part, :, pl.ds(j * 2 * LANES, 2 * LANES)], preferred_element_type=F32)
                for part in range(2)
            )
            for i in range(2):
                block = out[:, i * LANES : (i + 1) * LANES]
                block = block + pltpu.roll(block, 4, 0)
                contrib[s][pl.ds(2 * j + i, 4, stride=rows), :] = block[:4]
        for d in near_last(max(cross)) + [0]:
            for half in range(2):
                if d >= cross[half]:
                    continue
                for q, core in ((0, rep), (1, other)):
                    start = pl.multiple_of((half * 2 + core) * rows, rows)
                    land = pl.multiple_of(((d * 2 + rep) * 4 + target) * rows, rows)
                    if d == 0 and q == 0:
                        items[half, pl.ds(land, rows), :] = contrib[s][pl.ds(start, rows), :]
                        continue
                    remote(
                        contrib[s].at[pl.ds(start, rows), :], items.at[half, pl.ds(land, rows), :],
                        c_send, c_recv.at[half, min(d, 1)], along_cross(half, d), core,
                    ).start()

    order = near_last(lz) + [0]
    block = 2 * rows
    for half in range(2):
        drain(items.at[half, pl.ds(8 * rows, 8 * rows * (line - 1)), :], c_recv.at[half, 1])
        drain(items.at[half, pl.ds(pl.multiple_of(other * 4 * rows, rows), 4 * rows), :], c_recv.at[half, 0])
        slots = side[half] * lz * 2
        for j in range(0, rows, 2):
            value = jnp.concatenate(
                [
                    jnp.concatenate(
                        [items[half, pl.ds(d * 8 * rows + j + i, 8, stride=rows), :] for d in range(cross[half])],
                        axis=0,
                    )
                    for i in range(2)
                ],
                axis=1,
            )
            high = value.astype(BF16)
            low = (value - high.astype(F32)).astype(BF16)
            total = jnp.dot(
                placers[half], jnp.concatenate([high, low], axis=0), preferred_element_type=F32
            )
            for g in range(slots // 8):
                for i in range(2):
                    sums[half, pl.ds(g * 8 * rows + j + i, 8, stride=rows), :] = total[
                        g * 8 : g * 8 + 8, i * LANES : (i + 1) * LANES
                    ]
        for dz in order:
            for d in near_last(side[half]):
                remote(
                    sums.at[half, pl.ds((d * lz + dz) * block, block), :], terms.at[dz, half, d - 1],
                    r_send, r_recv.at[dz], along_side(half, d), rep,
                ).start()

    for dz in order:
        drain(terms.at[dz], r_recv.at[dz])
        for half in range(2):
            value = sums[half, pl.ds(dz * block, block), :]
            for d in range(1, side[half]):
                value = value + terms[dz, half, d - 1]
            (parts if dz == 0 else partial)[dz, half] = value
        if dz:
            remote(partial.at[dz], parts.at[dz], y_send, y_recv, chip(dz=dz), rep).start()
    drain(parts.at[pl.ds(1, lz - 1)], y_recv)
    for half in range(2):
        for cl in range(2):
            value = parts[0, half, pl.ds(cl * rows, rows), :]
            for dz in range(1, lz):
                value = value + parts[dz, half, pl.ds(cl * rows, rows), :]
            out_ref[cl, half] = value

    drain(pool.at[:, pl.ds(2, 2 * lz - 2)], z_send)
    drain(pool.at[:, pl.ds(2 * lz, 2 * lz * (line - 1))], d_send)
    drain(pool.at[:, pl.ds(0, 4 * (2 * line - 1))], s_send)
    drain(pool.at[:, pl.ds(0, 4 * (2 * line - 1))], c_send)
    drain(sums.at[:, pl.ds(lz * block, lz * block * (line - 1)), :], r_send)
    drain(parts.at[pl.ds(1, lz - 1)], y_send)


def local(dims, current, factors, ranks, pair_clusters):
    lz, ly, lx = dims
    unknowns = current.shape[3]
    rows = unknowns // LANES
    line = max(lx, ly)
    plane = 2 * lz * line
    dma = pltpu.SemaphoreType.DMA
    field = pl.pallas_call(
        functools.partial(kernel, dims),
        out_shape=jax.ShapeDtypeStruct((2, 2, rows, LANES), F32),
        in_specs=[pl.BlockSpec(memory_space=pltpu.HBM)] * 4,
        out_specs=pl.BlockSpec(memory_space=pltpu.VMEM),
        scratch_shapes=[
            pltpu.SMEM((2, pair_clusters.shape[0]), jnp.int32), pltpu.SMEM(ranks.shape, jnp.int32),
            pltpu.SMEM((16 * line,), jnp.int32),
            pltpu.VMEM((2, plane, rows, LANES), F32),
            pltpu.VMEM((2, line, 2, 4, rows, LANES), F32),
            [pltpu.VMEM((2, line, 2, rows, LANES), F32)] * 4,
            pltpu.VMEM((4, 8 * rows, LANES), F32),
            pltpu.VMEM((4, 2, 2 * RANK_ROWS, unknowns), BF16),
            pltpu.VMEM((4, 8, unknowns), BF16),
            [pltpu.VMEM((4 * rows, LANES), F32)] * 4,
            pltpu.VMEM((2, line * 8 * rows, LANES), F32),
            pltpu.VMEM((2, plane * rows, LANES), F32),
            pltpu.VMEM((lz, 2, line - 1, 2 * rows, LANES), F32),
            pltpu.VMEM((lz, 2, 2 * rows, LANES), F32),
            pltpu.VMEM((lz, 2, 2 * rows, LANES), F32),
            pltpu.VMEM((4, 2, RANK_ROWS, unknowns), F32),
            dma, dma((lz,)), dma, dma, dma, dma((4, 2)), dma, dma((2, 2)), dma, dma((lz,)), dma, dma,
            dma((4,)), dma((3,)),
        ],
        compiler_params=pltpu.CompilerParams(
            collective_id=0, has_side_effects=True, vmem_limit_bytes=48 * 1024 * 1024
        ),
    )(*[
        pltpu.with_memory_space_constraint(operand, pltpu.HBM)
        for operand in (pair_clusters.T, ranks, current.reshape(2, 2, rows, LANES), factors)
    ])
    return field.reshape(current.shape)


def solution(mesh, dims=(8, 4, 4)):
    placed = (
        P("clu", None, "rep", None),
        P(("clu", "rep"), None, None, None, None),
        P(("clu", "rep")),
        P(),
    )
    return jax.shard_map(
        functools.partial(local, dims), mesh=mesh, in_specs=placed,
        out_specs=P("clu", None, "rep", None), check_vma=False,
    )
```

```python
import functools

import jax
import jax.numpy as jnp
from jax import lax
from jax.experimental import pallas as pl
from jax.experimental.pallas import tpu as pltpu
from jax.sharding import PartitionSpec as P

MESH = pl.DeviceIdType.MESH
LANES = 128
RANK_ROWS = 48
F32, BF16 = jnp.float32, jnp.bfloat16


def near_last(count):
    return sorted(range(1, count), key=lambda d: (-min(d, count - d), d))


def kernel(
    dims, ids_hbm, ranks_hbm, cur_ref, fac_ref, out_ref,
    ids_ref, ranks_ref, slots_ref,
    pool, packed, refs, vecs, split, vec8, contrib, items, sums, terms, partial, parts, fac_buf,
    z_send, z_recv, d_send, d_recv, s_send, s_recv, c_send, c_recv, r_send, r_recv, y_send, y_recv, fac_sem, in_sem,
):
    lz, ly, lx = dims
    side = (ly, lx)
    cross = (lx, ly)
    rows = cur_ref.shape[2]
    line = lx
    clu, rep = lax.axis_index("clu"), lax.axis_index("rep")
    other = 1 - rep
    mx, my, mz = lax.rem(clu, lx), lax.rem(lax.div(clu, lx), ly), lax.div(clu, lx * ly)

    def chip(dx=0, dy=0, dz=0):
        x, y, z = lax.rem(mx + dx, lx), lax.rem(my + dy, ly), lax.rem(mz + dz, lz)
        return (z * ly + y) * lx + x

    def along_side(half, d):
        return chip(dy=d % ly) if half == 0 else chip(dx=d % lx)

    def along_cross(half, d):
        return chip(dx=d % lx) if half == 0 else chip(dy=d % ly)

    def ref_id(at, s):
        return ids_ref[s % 2, at * 4 + s // 2]

    def place(cid):
        bx, by = lx.bit_length() - 1, ly.bit_length() - 1
        return (cid >> 1) & (lx - 1), (cid >> (1 + bx)) & (ly - 1), cid >> (1 + bx + by), cid & 1

    def drain(ref, sem):
        pltpu.make_async_copy(ref, ref, sem).wait()

    def remote(src, dst, ssem, rsem, to, core):
        return pltpu.make_async_remote_copy(
            src_ref=src, dst_ref=dst, send_sem=ssem, recv_sem=rsem, device_id=(to, core), device_id_type=MESH
        )

    direct = [d for d in range(1, lz) if min(d, lz - d) <= 2]
    relays = [(3, 2, 1, (0, 1)), (5, 6, 7, (0, 1)), (4, 2, 2, (0,)), (4, 6, 6, (1,))] if lz == 8 else []
    barrier = pltpu.get_barrier_semaphore()
    peers = [(clu, other)]
    peers += [(chip(dz=d), rep) for d in direct]
    for half in range(2):
        for d in range(1, cross[half]):
            peers += [(along_cross(half, d), rep), (along_cross(half, d), other)]
    for peer in peers:
        pl.semaphore_signal(barrier, inc=1, device_id=peer, device_id_type=MESH)
    for half in range(2):
        pltpu.make_async_copy(cur_ref.at[:, half], pool.at[half, pl.ds(0, 2)], in_sem.at[0]).start()
    table_copies = [
        pltpu.make_async_copy(ids_hbm, ids_ref, in_sem.at[1]), pltpu.make_async_copy(ranks_hbm, ranks_ref, in_sem.at[2])
    ]
    for copy in table_copies:
        copy.start()
    fac_copies = []
    for p in range(2):
        for e in range(2):
            copy = pltpu.make_async_copy(
                fac_ref.at[p, e, :, pl.ds(0, RANK_ROWS), :], fac_buf.at[p * 2 + e], fac_sem.at[p * 2 + e]
            )
            copy.start()
            fac_copies.append(copy)
    drain(pool.at[:, pl.ds(0, 2)], in_sem.at[0])
    pl.semaphore_wait(barrier, len(peers))

    arrivals = {}

    def send_along_z(held, lands, step, halves, n):
        part = pl.ds(halves[0], len(halves))
        copy = remote(
            pool.at[part, pl.ds(2 * held, 2)], pool.at[part, pl.ds(2 * lands, 2)],
            z_send, z_recv.at[n], chip(dz=step), rep,
        )
        copy.start()
        arrivals.setdefault(lands, []).append(copy)

    arrival = [d for d in near_last(lz) if d in direct]
    for n, d in enumerate(arrival):
        send_along_z(0, d, d, (0, 1), n)
    arrival += [d for d in (3, 5, 4) if d not in direct and d < lz]

    def forward(dz):
        for d in near_last(max(side)):
            for half in range(2):
                if d >= side[half]:
                    continue
                remote(
                    pool.at[half, pl.ds(2 * dz, 2)], pool.at[half, pl.ds((d * lz + dz) * 2, 2)],
                    d_send, d_recv, along_side(half, d), rep,
                ).start()

    def split_factor(f):
        fac_copies[f].wait()
        for part in range(2):
            value = fac_buf[f, part]
            high = value.astype(BF16)
            split[f, 0, pl.ds(part * RANK_ROWS, RANK_ROWS), :] = high
            split[f, 1, pl.ds(part * RANK_ROWS, RANK_ROWS), :] = (value - high.astype(F32)).astype(BF16)

    def find_slots(half):
        for d in range(cross[half]):
            to = along_cross(half, d)
            for s in range(8):
                x, y, z, cl = place(ref_id(to, s))
                shift = (my - y if half == 0 else mx - x) & (side[half] - 1)
                slots_ref[(half * cross[half] + d) * 8 + s] = (shift * lz + ((mz - z) & (lz - 1))) * 2 + cl

    lane = lax.broadcasted_iota(jnp.int32, (8, LANES), 1)

    def make_placer(half):
        target = jnp.full((8, LANES), -1, jnp.int32)
        for d in range(cross[half]):
            source = along_cross(half, cross[half] - d)
            for s in range(8):
                x, y, z, cl = place(ref_id(source, s))
                mine = (x == mx) if half == 0 else (y == my)
                shift = (y - my if half == 0 else x - mx) & (side[half] - 1)
                slot = (shift * lz + ((z - mz) & (lz - 1))) * 2 + cl
                slot = jnp.where(mine, slot, -1)
                at = d * 8 + s
                target = jnp.where((lane == at) | (lane == at + 8 * cross[half]), slot, target)
        slots = side[half] * lz * 2
        wide = jnp.concatenate([target] * (slots // 8), axis=0)[:, : 16 * cross[half]]
        return jnp.where(lax.broadcasted_iota(jnp.int32, wide.shape, 0) == wide, 1.0, 0.0).astype(BF16)

    forward(0)
    for copy in table_copies:
        copy.wait()
    find_slots(0)
    find_slots(1)
    for n, dz in enumerate(arrival):
        for copy in arrivals[dz]:
            copy.wait_recv()
        for m, (lands, held, step, halves) in enumerate(relays):
            if held == dz:
                send_along_z(held, lands, step, halves, len(direct) + m)
        forward(dz)
        if n == 1 % len(arrival):
            split_factor(0)
            split_factor(1)
        if n == 3 % len(arrival):
            split_factor(2)
            split_factor(3)
    placers = [make_placer(0), make_placer(1)]
    drain(pool.at[:, pl.ds(2 * lz, 2 * lz * (line - 1))], d_recv)

    for s in range(4):
        for d in near_last(max(cross)) + [0]:
            for half in range(2):
                if d >= cross[half]:
                    continue
                for core in range(2):
                    packed[half, d, core, s] = pool[half, slots_ref[(half * cross[half] + d) * 8 + core * 4 + s]]
                for q, core in ((0, rep), (1, other)):
                    if d == 0 and q == 0:
                        refs[s][half, 0, rep] = packed[half, 0, rep, s]
                        continue
                    remote(
                        packed.at[half, d, core, s], refs[s].at[half, d, rep],
                        s_send, s_recv.at[s, min(d, 1)], along_cross(half, d), core,
                    ).start()

    row = lax.broadcasted_iota(jnp.int32, (8, LANES), 0)
    col = lax.broadcasted_iota(jnp.int32, (8, LANES), 1)
    first = row < 4
    sign = jnp.where(lax.rem(row, 4) < 2, -1.0, 1.0).astype(F32)
    def project(s):
        p, e = s // 2, s % 2
        x, y, z, cl = place(ids_ref[e, clu * 4 + rep * 2 + p])
        dx, dy = (mx - x) & (lx - 1), (my - y) & (ly - 1)
        for k in range(2):
            for half, d in ((0, dx), (1, dy)):
                value = refs[s][half, d, k]
                vecs[s, pl.ds((half * 2 + k) * rows, rows), :] = value
                vecs[s, pl.ds((4 + half * 2 + k) * rows, rows), :] = value
        for j in range(rows):
            value = vecs[s, pl.ds(j, 8, stride=rows), :]
            high = value.astype(BF16).astype(F32)
            vec8[s, :, pl.ds(j * LANES, LANES)] = jnp.where(first, high, value - high).astype(BF16)
        both = sum(
            lax.dot_general(vec8[s], split[s, part], (((1,), (1,)), ((), ())), preferred_element_type=F32)
            for part in range(2)
        )
        both = jnp.concatenate([both, jnp.zeros((8, LANES - 2 * RANK_ROWS), F32)], axis=1)
        both = both + pltpu.roll(both, 4, 0)
        t = both + sign * pltpu.roll(pltpu.roll(both, LANES - RANK_ROWS, 1), 2, 0)
        t = jnp.where(col < jnp.minimum(ranks_ref[p], RANK_ROWS), t, 0.0)
        t = t + pltpu.roll(sign * pltpu.roll(t, 2, 0), RANK_ROWS, 1)
        high = t.astype(BF16).astype(F32)
        return jnp.where(first, high, t - high).astype(BF16)[:, : 2 * RANK_ROWS]

    def expand(s, t):
        target = s ^ 1
        for j in range(rows // 2):
            out = sum(
                jnp.dot(t, split[target, part, :, pl.ds(j * 2 * LANES, 2 * LANES)], preferred_element_type=F32)
                for part in range(2)
            )
            for i in range(2):
                block = out[:, i * LANES : (i + 1) * LANES]
                block = block + pltpu.roll(block, 4, 0)
                contrib[s][pl.ds(2 * j + i, 4, stride=rows), :] = block[:4]

    def send_back(s):
        target = s ^ 1
        for d in near_last(max(cross)) + [0]:
            for half in range(2):
                if d >= cross[half]:
                    continue
                for q, core in ((0, rep), (1, other)):
                    start = pl.multiple_of((half * 2 + core) * rows, rows)
                    land = pl.multiple_of(((d * 2 + rep) * 4 + target) * rows, rows)
                    if d == 0 and q == 0:
                        items[half, pl.ds(land, rows), :] = contrib[s][pl.ds(start, rows), :]
                        continue
                    remote(
                        contrib[s].at[pl.ds(start, rows), :], items.at[half, pl.ds(land, rows), :],
                        c_send, c_recv.at[half, min(d, 1)], along_cross(half, d), core,
                    ).start()

    projected = {}
    for s in range(5):
        if s < 4:
            drain(refs[s].at[:, pl.ds(1, line - 1)], s_recv.at[s, 1])
            drain(refs[s].at[:, 0, other], s_recv.at[s, 0])
            projected[s] = project(s)
        if s > 0:
            expand(s - 1, projected[s - 1])
            send_back(s - 1)

    order = near_last(lz) + [0]
    block = 2 * rows
    for half in range(2):
        drain(items.at[half, pl.ds(8 * rows, 8 * rows * (line - 1)), :], c_recv.at[half, 1])
        drain(items.at[half, pl.ds(pl.multiple_of(other * 4 * rows, rows), 4 * rows), :], c_recv.at[half, 0])
        slots = side[half] * lz * 2
        for j in range(0, rows, 2):
            value = jnp.concatenate(
                [
                    jnp.concatenate(
                        [items[half, pl.ds(d * 8 * rows + j + i, 8, stride=rows), :] for d in range(cross[half])],
                        axis=0,
                    )
                    for i in range(2)
                ],
                axis=1,
            )
            high = value.astype(BF16)
            low = (value - high.astype(F32)).astype(BF16)
            total = jnp.dot(
                placers[half], jnp.concatenate([high, low], axis=0), preferred_element_type=F32
            )
            for g in range(slots // 8):
                for i in range(2):
                    sums[half, pl.ds(g * 8 * rows + j + i, 8, stride=rows), :] = total[
                        g * 8 : g * 8 + 8, i * LANES : (i + 1) * LANES
                    ]
        for dz in order:
            for d in near_last(side[half]):
                remote(
                    sums.at[half, pl.ds((d * lz + dz) * block, block), :], terms.at[dz, half, d - 1],
                    r_send, r_recv.at[dz], along_side(half, d), rep,
                ).start()

    for dz in order:
        drain(terms.at[dz], r_recv.at[dz])
        for half in range(2):
            value = sums[half, pl.ds(dz * block, block), :]
            for d in range(1, side[half]):
                value = value + terms[dz, half, d - 1]
            (parts if dz == 0 else partial)[dz, half] = value
        if dz:
            remote(partial.at[dz], parts.at[dz], y_send, y_recv, chip(dz=dz), rep).start()
    drain(parts.at[pl.ds(1, lz - 1)], y_recv)
    for half in range(2):
        for cl in range(2):
            value = parts[0, half, pl.ds(cl * rows, rows), :]
            for dz in range(1, lz):
                value = value + parts[dz, half, pl.ds(cl * rows, rows), :]
            out_ref[cl, half] = value

    drain(pool.at[:, pl.ds(2, 2 * lz - 2)], z_send)
    drain(pool.at[:, pl.ds(2 * lz, 2 * lz * (line - 1))], d_send)
    drain(pool.at[:, pl.ds(0, 4 * (2 * line - 1))], s_send)
    drain(pool.at[:, pl.ds(0, 4 * (2 * line - 1))], c_send)
    drain(sums.at[:, pl.ds(lz * block, lz * block * (line - 1)), :], r_send)
    drain(parts.at[pl.ds(1, lz - 1)], y_send)


def local(dims, current, factors, ranks, pair_clusters):
    lz, ly, lx = dims
    unknowns = current.shape[3]
    rows = unknowns // LANES
    line = max(lx, ly)
    plane = 2 * lz * line
    dma = pltpu.SemaphoreType.DMA
    field = pl.pallas_call(
        functools.partial(kernel, dims),
        out_shape=jax.ShapeDtypeStruct((2, 2, rows, LANES), F32),
        in_specs=[pl.BlockSpec(memory_space=pltpu.HBM)] * 4,
        out_specs=pl.BlockSpec(memory_space=pltpu.VMEM),
        scratch_shapes=[
            pltpu.SMEM((2, pair_clusters.shape[0]), jnp.int32), pltpu.SMEM(ranks.shape, jnp.int32),
            pltpu.SMEM((16 * line,), jnp.int32),
            pltpu.VMEM((2, plane, rows, LANES), F32),
            pltpu.VMEM((2, line, 2, 4, rows, LANES), F32),
            [pltpu.VMEM((2, line, 2, rows, LANES), F32)] * 4,
            pltpu.VMEM((4, 8 * rows, LANES), F32),
            pltpu.VMEM((4, 2, 2 * RANK_ROWS, unknowns), BF16),
            pltpu.VMEM((4, 8, unknowns), BF16),
            [pltpu.VMEM((4 * rows, LANES), F32)] * 4,
            pltpu.VMEM((2, line * 8 * rows, LANES), F32),
            pltpu.VMEM((2, plane * rows, LANES), F32),
            pltpu.VMEM((lz, 2, line - 1, 2 * rows, LANES), F32),
            pltpu.VMEM((lz, 2, 2 * rows, LANES), F32),
            pltpu.VMEM((lz, 2, 2 * rows, LANES), F32),
            pltpu.VMEM((4, 2, RANK_ROWS, unknowns), F32),
            dma, dma((lz,)), dma, dma, dma, dma((4, 2)), dma, dma((2, 2)), dma, dma((lz,)), dma, dma,
            dma((4,)), dma((3,)),
        ],
        compiler_params=pltpu.CompilerParams(
            collective_id=0, has_side_effects=True, vmem_limit_bytes=48 * 1024 * 1024
        ),
    )(*[
        pltpu.with_memory_space_constraint(operand, pltpu.HBM)
        for operand in (pair_clusters.T, ranks, current.reshape(2, 2, rows, LANES), factors)
    ])
    return field.reshape(current.shape)


def solution(mesh, dims=(8, 4, 4)):
    placed = (
        P("clu", None, "rep", None),
        P(("clu", "rep"), None, None, None, None),
        P(("clu", "rep")),
        P(),
    )
    return jax.shard_map(
        functools.partial(local, dims), mesh=mesh, in_specs=placed,
        out_specs=P("clu", None, "rep", None), check_vma=False,
    )
```

```python
import functools

import jax
import jax.numpy as jnp
from jax import lax
from jax.experimental import pallas as pl
from jax.experimental.pallas import tpu as pltpu
from jax.sharding import PartitionSpec as P

MESH = pl.DeviceIdType.MESH
LANES = 128
RANK_ROWS = 48
F32, BF16 = jnp.float32, jnp.bfloat16


def near_last(count):
    return sorted(range(1, count), key=lambda d: (-min(d, count - d), d))


def kernel(
    dims, ids_hbm, ranks_hbm, cur_ref, fac_ref, out_ref,
    ids_ref, ranks_ref, slots_ref,
    pool, packed, refs, vecs, split, vec8, contrib, items, sums, terms, partial, parts, fac_buf,
    z_send, z_recv, d_send, d_recv, s_send, s_recv, c_send, c_recv, r_send, r_recv, y_send, y_recv, fac_sem, in_sem,
):
    lz, ly, lx = dims
    side = (ly, lx)
    cross = (lx, ly)
    rows = cur_ref.shape[2]
    line = lx
    clu, rep = lax.axis_index("clu"), lax.axis_index("rep")
    other = 1 - rep
    mx, my, mz = lax.rem(clu, lx), lax.rem(lax.div(clu, lx), ly), lax.div(clu, lx * ly)

    def chip(dx=0, dy=0, dz=0):
        x, y, z = lax.rem(mx + dx, lx), lax.rem(my + dy, ly), lax.rem(mz + dz, lz)
        return (z * ly + y) * lx + x

    def along_side(half, d):
        return chip(dy=d % ly) if half == 0 else chip(dx=d % lx)

    def along_cross(half, d):
        return chip(dx=d % lx) if half == 0 else chip(dy=d % ly)

    def ref_id(at, s):
        return ids_ref[s % 2, at * 4 + s // 2]

    def place(cid):
        bx, by = lx.bit_length() - 1, ly.bit_length() - 1
        return (cid >> 1) & (lx - 1), (cid >> (1 + bx)) & (ly - 1), cid >> (1 + bx + by), cid & 1

    def drain(ref, sem):
        pltpu.make_async_copy(ref, ref, sem).wait()

    def remote(src, dst, ssem, rsem, to, core):
        return pltpu.make_async_remote_copy(
            src_ref=src, dst_ref=dst, send_sem=ssem, recv_sem=rsem, device_id=(to, core), device_id_type=MESH
        )

    direct = [d for d in range(1, lz) if min(d, lz - d) <= 2]
    relays = [(3, 2, 1, (0, 1)), (5, 6, 7, (0, 1)), (4, 2, 2, (0,)), (4, 6, 6, (1,))] if lz == 8 else []
    barrier = pltpu.get_barrier_semaphore()
    peers = [(clu, other)]
    peers += [(chip(dz=d), rep) for d in direct]
    for half in range(2):
        for d in range(1, cross[half]):
            peers += [(along_cross(half, d), rep), (along_cross(half, d), other)]
    for peer in peers:
        pl.semaphore_signal(barrier, inc=1, device_id=peer, device_id_type=MESH)
    for half in range(2):
        pltpu.make_async_copy(cur_ref.at[:, half], pool.at[half, pl.ds(0, 2)], in_sem.at[0]).start()
    table_copies = [
        pltpu.make_async_copy(ids_hbm, ids_ref, in_sem.at[1]), pltpu.make_async_copy(ranks_hbm, ranks_ref, in_sem.at[2])
    ]
    for copy in table_copies:
        copy.start()
    fac_copies = []
    for p in range(2):
        for e in range(2):
            copy = pltpu.make_async_copy(
                fac_ref.at[p, e, :, pl.ds(0, RANK_ROWS), :], fac_buf.at[p * 2 + e], fac_sem.at[p * 2 + e]
            )
            copy.start()
            fac_copies.append(copy)
    drain(pool.at[:, pl.ds(0, 2)], in_sem.at[0])
    pl.semaphore_wait(barrier, len(peers))

    arrivals = {}

    def send_along_z(held, lands, step, halves, n):
        part = pl.ds(halves[0], len(halves))
        copy = remote(
            pool.at[part, pl.ds(2 * held, 2)], pool.at[part, pl.ds(2 * lands, 2)],
            z_send, z_recv.at[n], chip(dz=step), rep,
        )
        copy.start()
        arrivals.setdefault(lands, []).append(copy)

    arrival = [d for d in near_last(lz) if d in direct]
    for n, d in enumerate(arrival):
        send_along_z(0, d, d, (0, 1), n)
    arrival += [d for d in (3, 5, 4) if d not in direct and d < lz]

    def forward(dz):
        for d in near_last(max(side)):
            for half in range(2):
                if d >= side[half]:
                    continue
                remote(
                    pool.at[half, pl.ds(2 * dz, 2)], pool.at[half, pl.ds((d * lz + dz) * 2, 2)],
                    d_send, d_recv, along_side(half, d), rep,
                ).start()

    def split_factor(f):
        fac_copies[f].wait()
        for part in range(2):
            value = fac_buf[f, part]
            high = value.astype(BF16)
            split[f, 0, pl.ds(part * RANK_ROWS, RANK_ROWS), :] = high
            split[f, 1, pl.ds(part * RANK_ROWS, RANK_ROWS), :] = (value - high.astype(F32)).astype(BF16)

    def find_slots(half):
        for d in range(cross[half]):
            to = along_cross(half, d)
            for s in range(8):
                x, y, z, cl = place(ref_id(to, s))
                shift = (my - y if half == 0 else mx - x) & (side[half] - 1)
                slots_ref[(half * cross[half] + d) * 8 + s] = (shift * lz + ((mz - z) & (lz - 1))) * 2 + cl

    lane = lax.broadcasted_iota(jnp.int32, (8, LANES), 1)

    def make_placer(half):
        target = jnp.full((8, LANES), -1, jnp.int32)
        for d in range(cross[half]):
            source = along_cross(half, cross[half] - d)
            for s in range(8):
                x, y, z, cl = place(ref_id(source, s))
                mine = (x == mx) if half == 0 else (y == my)
                shift = (y - my if half == 0 else x - mx) & (side[half] - 1)
                slot = (shift * lz + ((z - mz) & (lz - 1))) * 2 + cl
                slot = jnp.where(mine, slot, -1)
                at = d * 8 + s
                target = jnp.where((lane == at) | (lane == at + 8 * cross[half]), slot, target)
        slots = side[half] * lz * 2
        wide = jnp.concatenate([target] * (slots // 8), axis=0)[:, : 16 * cross[half]]
        return jnp.where(lax.broadcasted_iota(jnp.int32, wide.shape, 0) == wide, 1.0, 0.0).astype(BF16)

    forward(0)
    for copy in table_copies:
        copy.wait()
    find_slots(0)
    find_slots(1)
    for n, dz in enumerate(arrival):
        for copy in arrivals[dz]:
            copy.wait_recv()
        for m, (lands, held, step, halves) in enumerate(relays):
            if held == dz:
                send_along_z(held, lands, step, halves, len(direct) + m)
        forward(dz)
        if n == 1 % len(arrival):
            split_factor(0)
            split_factor(1)
        if n == 3 % len(arrival):
            split_factor(2)
            split_factor(3)
    placers = [make_placer(0), make_placer(1)]
    drain(pool.at[:, pl.ds(2 * lz, 2 * lz * (line - 1))], d_recv)

    for s in range(4):
        for d in near_last(max(cross)) + [0]:
            for half in range(2):
                if d >= cross[half]:
                    continue
                for core in range(2):
                    packed[half, d, core, s] = pool[half, slots_ref[(half * cross[half] + d) * 8 + core * 4 + s]]
                for q, core in ((0, rep), (1, other)):
                    if d == 0 and q == 0:
                        refs[s][half, 0, rep] = packed[half, 0, rep, s]
                        continue
                    remote(
                        packed.at[half, d, core, s], refs[s].at[half, d, rep],
                        s_send, s_recv.at[s, min(d, 1)], along_cross(half, d), core,
                    ).start()

    row = lax.broadcasted_iota(jnp.int32, (8, LANES), 0)
    col = lax.broadcasted_iota(jnp.int32, (8, LANES), 1)
    first = row < 4
    sign = jnp.where(lax.rem(row, 4) < 2, -1.0, 1.0).astype(F32)
    def project(s):
        p, e = s // 2, s % 2
        x, y, z, cl = place(ids_ref[e, clu * 4 + rep * 2 + p])
        dx, dy = (mx - x) & (lx - 1), (my - y) & (ly - 1)
        for k in range(2):
            for half, d in ((0, dx), (1, dy)):
                value = refs[s][half, d, k]
                vecs[s, pl.ds((half * 2 + k) * rows, rows), :] = value
                vecs[s, pl.ds((4 + half * 2 + k) * rows, rows), :] = value
        for j in range(rows):
            value = vecs[s, pl.ds(j, 8, stride=rows), :]
            high = value.astype(BF16).astype(F32)
            vec8[s, :, pl.ds(j * LANES, LANES)] = jnp.where(first, high, value - high).astype(BF16)
        both = sum(
            lax.dot_general(vec8[s], split[s, part], (((1,), (1,)), ((), ())), preferred_element_type=F32)
            for part in range(2)
        )
        both = jnp.concatenate([both, jnp.zeros((8, LANES - 2 * RANK_ROWS), F32)], axis=1)
        both = both + pltpu.roll(both, 4, 0)
        t = both + sign * pltpu.roll(pltpu.roll(both, LANES - RANK_ROWS, 1), 2, 0)
        t = jnp.where(col < jnp.minimum(ranks_ref[p], RANK_ROWS), t, 0.0)
        t = t + pltpu.roll(sign * pltpu.roll(t, 2, 0), RANK_ROWS, 1)
        high = t.astype(BF16).astype(F32)
        return jnp.where(first, high, t - high).astype(BF16)[:, : 2 * RANK_ROWS]

    def expand(s, t):
        target = s ^ 1
        for j in range(rows // 2):
            out = sum(
                jnp.dot(t, split[target, part, :, pl.ds(j * 2 * LANES, 2 * LANES)], preferred_element_type=F32)
                for part in range(2)
            )
            for i in range(2):
                block = out[:, i * LANES : (i + 1) * LANES]
                block = block + pltpu.roll(block, 4, 0)
                contrib[s][pl.ds(2 * j + i, 4, stride=rows), :] = block[:4]

    def send_back(s):
        target = s ^ 1
        for d in near_last(max(cross)) + [0]:
            for half in range(2):
                if d >= cross[half]:
                    continue
                for q, core in ((0, rep), (1, other)):
                    start = pl.multiple_of((half * 2 + core) * rows, rows)
                    land = pl.multiple_of(((d * 2 + rep) * 4 + target) * rows, rows)
                    if d == 0 and q == 0:
                        items[half, pl.ds(land, rows), :] = contrib[s][pl.ds(start, rows), :]
                        continue
                    remote(
                        contrib[s].at[pl.ds(start, rows), :], items.at[half, pl.ds(land, rows), :],
                        c_send, c_recv.at[half, min(d, 1)], along_cross(half, d), core,
                    ).start()

    projected = {}
    for s in range(5):
        if s < 4:
            drain(refs[s].at[:, pl.ds(1, line - 1)], s_recv.at[s, 1])
            drain(refs[s].at[:, 0, other], s_recv.at[s, 0])
            projected[s] = project(s)
        if s > 0:
            expand(s - 1, projected[s - 1])
            send_back(s - 1)

    order = near_last(lz) + [0]
    block = 2 * rows

    def send_sums(half, dz):
        for d in near_last(line):
            remote(
                sums.at[half, pl.ds((d * lz + dz) * block, block), :], terms.at[dz, half, d - 1],
                r_send, r_recv.at[dz], along_side(half, d), rep,
            ).start()

    for half in range(2):
        drain(items.at[half, pl.ds(8 * rows, 8 * rows * (line - 1)), :], c_recv.at[half, 1])
        drain(items.at[half, pl.ds(pl.multiple_of(other * 4 * rows, rows), 4 * rows), :], c_recv.at[half, 0])
        slots = side[half] * lz * 2
        for j in range(0, rows, 2):
            value = jnp.concatenate(
                [
                    jnp.concatenate(
                        [items[half, pl.ds(d * 8 * rows + j + i, 8, stride=rows), :] for d in range(cross[half])],
                        axis=0,
                    )
                    for i in range(2)
                ],
                axis=1,
            )
            high = value.astype(BF16)
            low = (value - high.astype(F32)).astype(BF16)
            total = jnp.dot(
                placers[half], jnp.concatenate([high, low], axis=0), preferred_element_type=F32
            )
            for g in range(slots // 8):
                for i in range(2):
                    sums[half, pl.ds(g * 8 * rows + j + i, 8, stride=rows), :] = total[
                        g * 8 : g * 8 + 8, i * LANES : (i + 1) * LANES
                    ]
        if half == 0:
            for dz in order[:2]:
                send_sums(half, dz)
    for dz in order[:2]:
        send_sums(1, dz)
    for dz in order[2:]:
        send_sums(0, dz)
        send_sums(1, dz)

    for dz in order:
        drain(terms.at[dz], r_recv.at[dz])
        for half in range(2):
            value = sums[half, pl.ds(dz * block, block), :]
            for d in range(1, side[half]):
                value = value + terms[dz, half, d - 1]
            (parts if dz == 0 else partial)[dz, half] = value
        if dz:
            remote(partial.at[dz], parts.at[dz], y_send, y_recv, chip(dz=dz), rep).start()
    drain(parts.at[pl.ds(1, lz - 1)], y_recv)
    for half in range(2):
        for cl in range(2):
            value = parts[0, half, pl.ds(cl * rows, rows), :]
            for dz in range(1, lz):
                value = value + parts[dz, half, pl.ds(cl * rows, rows), :]
            out_ref[cl, half] = value

    drain(pool.at[:, pl.ds(2, 2 * lz - 2)], z_send)
    drain(pool.at[:, pl.ds(2 * lz, 2 * lz * (line - 1))], d_send)
    drain(pool.at[:, pl.ds(0, 4 * (2 * line - 1))], s_send)
    drain(pool.at[:, pl.ds(0, 4 * (2 * line - 1))], c_send)
    drain(sums.at[:, pl.ds(lz * block, lz * block * (line - 1)), :], r_send)
    drain(parts.at[pl.ds(1, lz - 1)], y_send)


def local(dims, current, factors, ranks, pair_clusters):
    lz, ly, lx = dims
    unknowns = current.shape[3]
    rows = unknowns // LANES
    line = max(lx, ly)
    plane = 2 * lz * line
    dma = pltpu.SemaphoreType.DMA
    field = pl.pallas_call(
        functools.partial(kernel, dims),
        out_shape=jax.ShapeDtypeStruct((2, 2, rows, LANES), F32),
        in_specs=[pl.BlockSpec(memory_space=pltpu.HBM)] * 4,
        out_specs=pl.BlockSpec(memory_space=pltpu.VMEM),
        scratch_shapes=[
            pltpu.SMEM((2, pair_clusters.shape[0]), jnp.int32), pltpu.SMEM(ranks.shape, jnp.int32),
            pltpu.SMEM((16 * line,), jnp.int32),
            pltpu.VMEM((2, plane, rows, LANES), F32),
            pltpu.VMEM((2, line, 2, 4, rows, LANES), F32),
            [pltpu.VMEM((2, line, 2, rows, LANES), F32)] * 4,
            pltpu.VMEM((4, 8 * rows, LANES), F32),
            pltpu.VMEM((4, 2, 2 * RANK_ROWS, unknowns), BF16),
            pltpu.VMEM((4, 8, unknowns), BF16),
            [pltpu.VMEM((4 * rows, LANES), F32)] * 4,
            pltpu.VMEM((2, line * 8 * rows, LANES), F32),
            pltpu.VMEM((2, plane * rows, LANES), F32),
            pltpu.VMEM((lz, 2, line - 1, 2 * rows, LANES), F32),
            pltpu.VMEM((lz, 2, 2 * rows, LANES), F32),
            pltpu.VMEM((lz, 2, 2 * rows, LANES), F32),
            pltpu.VMEM((4, 2, RANK_ROWS, unknowns), F32),
            dma, dma((lz,)), dma, dma, dma, dma((4, 2)), dma, dma((2, 2)), dma, dma((lz,)), dma, dma,
            dma((4,)), dma((3,)),
        ],
        compiler_params=pltpu.CompilerParams(
            collective_id=0, has_side_effects=True, vmem_limit_bytes=48 * 1024 * 1024
        ),
    )(*[
        pltpu.with_memory_space_constraint(operand, pltpu.HBM)
        for operand in (pair_clusters.T, ranks, current.reshape(2, 2, rows, LANES), factors)
    ])
    return field.reshape(current.shape)


def solution(mesh, dims=(8, 4, 4)):
    placed = (
        P("clu", None, "rep", None),
        P(("clu", "rep"), None, None, None, None),
        P(("clu", "rep")),
        P(),
    )
    return jax.shard_map(
        functools.partial(local, dims), mesh=mesh, in_specs=placed,
        out_specs=P("clu", None, "rep", None), check_vma=False,
    )
```
